1024 devices in a mesh: section: 4 (over y), seq: 8 (over x, core), tp: 32 (over z).
Axes of the slice: x: 4, y: 4, z: 32, core: 2. Of those that a mesh axis runs over, the one named last changes fastest.
Arguments:
- waiting_batchlets: bfloat16 [4, 1024, 4096], P('section', 'seq', 'tp'), may hold values from -6 to 6
- arriving_batchlet: bfloat16 [1024, 4096], P('seq', 'tp'), may hold values from -6 to 6
- entry_rescale_factor: float32 [4, 4096], P('section'), may hold values from 0.25 to 1.75
- entry_projection_matrix: bfloat16 [4, 4096, 16384], P('section', None, 'tp'), may hold values from -0.09375 to 0.09375
- timescale_projection: bfloat16 [4, 4096, 128], P('section', None, 'tp'), may hold values from -0.09375 to 0.09375
- timescale_offset: float32 [4, 128], P('section', 'tp'), may hold values from -1 to 1
- channel_forgetting_rate: int32 [4, 128], P('section', 'tp'), may hold values from 0 to 7
- state_read_write_matrix: bfloat16 [4, 4096, 4096], P('section', None, 'tp'), may hold values from -0.0234375 to 0.0234375
- direct_passthrough: float32 [4, 128], P('section', 'tp'), may hold values from 0.5 to 1.5
- closing_rescale_factor: float32 [4, 8192], P('section', 'tp'), may hold values from 0.25 to 1.75
- closing_projection_matrix: bfloat16 [4, 8192, 4096], P('section', 'tp'), may hold values from -0.0625 to 0.0625
Outputs:
- section_out: bfloat16 [4, 1024, 4096], P('section', 'seq', 'tp')
The draws below stay inside these ranges and needn't reach their ends.
All inputs are finite; a program needn't handle non-finite values.
Results may differ from the reference program's by a relative error of at most 0.03.
Values may be sent and summed in bfloat16 or wider, within the bound.
No kernel may reach another device: no remote copies, remote signals or barrier semaphores. Data moves between devices by JAX's collectives and lax.ppermute only.
A program may use at most 128 MiB of HBM per device.

```python
import jax
import jax.numpy as jnp
from jax import lax

HIDDEN_DIMENSION = 4096
HEADS = 128
NGROUPS = 8
HEAD_DIM = 64
STATE = 256
BLOCK_COUNT = 4
BATCHLET_LENGTH = 1024
INNER = 8192
GROUP = 1024
N_TP = 32


def with_ends(array, rng, low, largest):
    longest = array.shape.index(max(array.shape))
    spots = []
    for shift in (0, 1):
        where = [jax.random.randint(jax.random.fold_in(rng, axis), (), 0, length) for axis, length in enumerate(array.shape)]
        where[longest] = (where[longest] + shift) % array.shape[longest]
        spots.append(tuple(where))
    return array.at[spots[0]].set(low).at[spots[1]].set(largest)


def block_levels(key, extent, cuts, low, largest):
    def one(position, shards_of):
        draws = jax.random.uniform(jax.random.fold_in(jax.random.fold_in(key, 6), position), (shards_of,), jnp.float32, low / len(cuts), largest / len(cuts))
        return jnp.repeat(jnp.exp(draws), extent[position] // shards_of).reshape((-1,) + (1,) * (len(extent) - position - 1))

    level = one(*cuts[0])
    for cut in cuts[1:]:
        level = level * one(*cut)
    return level


def bell_draw(stream_key, extent, width, bound, shards=(), kind=jnp.bfloat16):
    entries = width * jax.random.normal(stream_key, extent, jnp.float32)
    if shards:
        entries = entries * block_levels(stream_key, extent, shards, -0.22, 0.18)
    return jnp.clip(entries, -bound, bound).astype(kind)


def setup_inputs(seed: int = 0) -> dict:
    seeds = jax.random.split(jax.random.key(seed), 12)
    return {
        "waiting_batchlets": bell_draw(seeds[0], (BLOCK_COUNT, BATCHLET_LENGTH, HIDDEN_DIMENSION), 1.0, 6.0, ((0, 4), (1, 8), (2, 32))),
        "arriving_batchlet": bell_draw(seeds[1], (BATCHLET_LENGTH, HIDDEN_DIMENSION), 1.0, 6.0, ((0, 8), (1, 32))),
        "entry_rescale_factor": jnp.clip(1.0 + 0.15 * jax.random.normal(seeds[2], (BLOCK_COUNT, HIDDEN_DIMENSION), jnp.float32), 0.25, 1.75),
        "entry_projection_matrix": bell_draw(seeds[3], (BLOCK_COUNT, HIDDEN_DIMENSION, 2 * INNER), HIDDEN_DIMENSION ** -0.5, 0.09375, ((0, 4), (2, 32))),
        "timescale_projection": bell_draw(seeds[4], (BLOCK_COUNT, HIDDEN_DIMENSION, HEADS), HIDDEN_DIMENSION ** -0.5, 0.09375, ((0, 4), (2, 32))),
        "timescale_offset": jnp.clip(jax.random.uniform(seeds[5], (BLOCK_COUNT, HEADS), jnp.float32, -1.0, 1.0) * block_levels(seeds[5], (BLOCK_COUNT, HEADS), ((0, 4), (1, 32)), -0.4, 0.0), -1.0, 1.0),
        "channel_forgetting_rate": with_ends(jax.random.randint(seeds[6], (BLOCK_COUNT, HEADS), 0, 8), jax.random.fold_in(seeds[6], 1), 0, 7).astype(jnp.int32),
        "state_read_write_matrix": bell_draw(seeds[7], (BLOCK_COUNT, HIDDEN_DIMENSION, NGROUPS * 2 * STATE), (HIDDEN_DIMENSION * 16) ** -0.5, 0.0234375, ((0, 4), (2, 32))),
        "direct_passthrough": jnp.clip(0.5 + 1.0 * jax.random.uniform(seeds[8], (BLOCK_COUNT, HEADS), jnp.float32) ** block_levels(seeds[8], (BLOCK_COUNT, HEADS), ((0, 4), (1, 32)), -0.2, 0.2), 0.5, 1.5),
        "closing_rescale_factor": jnp.clip(1.0 + 0.15 * jax.random.normal(seeds[9], (BLOCK_COUNT, INNER), jnp.float32), 0.25, 1.75),
        "closing_projection_matrix": bell_draw(seeds[10], (BLOCK_COUNT, INNER, HIDDEN_DIMENSION), INNER ** -0.5, 0.0625, ((0, 4), (1, 32))),
    }


def mixer(resid, gain, w_inp, w_step, bias, code, w_shared, skip_coef, o_gain, w_outp):
    count = resid.shape[0]
    values = resid.astype(jnp.float32)
    inv = lax.rsqrt(lax.optimization_barrier(jnp.mean(values * values, axis=1, keepdims=True)) + 1e-05)
    scaled = (values * gain[None, :]).astype(jnp.bfloat16)
    proj = jnp.dot(scaled, w_inp, preferred_element_type=jnp.float32) * inv
    pairs = proj.reshape(count, HEADS, 2, HEAD_DIM)
    xs = pairs[:, :, 0, :]
    gates = pairs[:, :, 1, :]
    step = jax.nn.softplus(jnp.dot(scaled, w_step, preferred_element_type=jnp.float32) * inv + bias[None, :])
    shared_low = (jnp.dot(scaled, w_shared, preferred_element_type=jnp.float32) * inv).astype(jnp.bfloat16)
    shared_low = lax.optimization_barrier(shared_low)
    shared = jnp.transpose(shared_low.astype(jnp.float32).reshape(count, 2 * STATE, NGROUPS), (0, 2, 1))
    rates = 0.0005 * jnp.exp2(code.astype(jnp.float32))
    cum = jnp.cumsum(-(step * rates[None, :]), axis=0)
    xdt = xs * step[:, :, None]
    lower = jnp.arange(count)[:, None] >= jnp.arange(count)[None, :]
    per_group = HEADS // NGROUPS

    def one_head(head):
        group_id = (head // per_group).astype(jnp.int32)
        rows = lax.dynamic_index_in_dim(shared, group_id, 1, keepdims=False)
        bmat = rows[:, :STATE]
        cmat = rows[:, STATE:]
        scores = jnp.dot(cmat, bmat.T, precision=lax.Precision.HIGHEST)
        column = lax.dynamic_index_in_dim(cum, head, 1, keepdims=False)
        inputs = lax.dynamic_index_in_dim(xdt, head, 1, keepdims=False)
        decay = jnp.where(lower, jnp.exp(jnp.minimum(column[:, None] - column[None, :], 0.0)), 0.0)
        return jnp.dot(decay * scores, inputs, precision=lax.Precision.HIGHEST)
    intra = lax.map(one_head, jnp.arange(HEADS, dtype=jnp.int32))
    mixed = jnp.transpose(intra, (1, 0, 2)) + skip_coef[None, :, None] * xs
    gated = (mixed * jax.nn.silu(gates)).reshape(count, INNER // GROUP, GROUP)
    gated = gated * lax.rsqrt(lax.optimization_barrier(jnp.mean(gated * gated, axis=2, keepdims=True)) + 1e-05)
    normed = (gated.reshape(count, INNER) * o_gain[None, :]).astype(jnp.bfloat16)
    block = INNER // N_TP

    def add_block(total, index):
        start = (index * block).astype(jnp.int32)
        left = lax.dynamic_slice_in_dim(normed, start, block, 1)
        right = lax.dynamic_slice_in_dim(w_outp, start, block, 0)
        part = jnp.dot(left, right, preferred_element_type=jnp.float32).astype(jnp.bfloat16)
        part = lax.optimization_barrier(part)
        return (total + part.astype(jnp.float32), None)
    summed, _ = lax.scan(add_block, jnp.zeros((count, HIDDEN_DIMENSION), jnp.float32), jnp.arange(N_TP, dtype=jnp.int32))
    return (values + summed).astype(jnp.bfloat16)

def reference(waiting_batchlets, arriving_batchlet, entry_rescale_factor, entry_projection_matrix, timescale_projection, timescale_offset, channel_forgetting_rate, state_read_write_matrix, direct_passthrough, closing_rescale_factor, closing_projection_matrix):

    def block_ordinal(block_counter, resid):
        return mixer(resid, entry_rescale_factor[block_counter], entry_projection_matrix[block_counter], timescale_projection[block_counter], timescale_offset[block_counter], channel_forgetting_rate[block_counter], state_read_write_matrix[block_counter], direct_passthrough[block_counter], closing_rescale_factor[block_counter], closing_projection_matrix[block_counter])
    results = [block_ordinal(0, arriving_batchlet)]
    for block_counter in range(1, BLOCK_COUNT):
        prior_round_produced = block_ordinal(block_counter - 1, waiting_batchlets[block_counter - 1])
        results.append(block_ordinal(block_counter, prior_round_produced))
    return jnp.stack(results)
```

```python
import jax
import jax.numpy as jnp
from jax import lax
from jax.sharding import Mesh
from jax.sharding import PartitionSpec as P

HEAD_DIM = 64
SEQ = ("seq_0", "seq_1")
TP = ("tp_hi", "tp_lo")
BF = jnp.bfloat16
F32 = jnp.float32


def swap(value, axis):
    return lax.all_to_all(value, axis, 0, 0, tiled=True)


def spread(value, axis):
    return swap(jnp.broadcast_to(value[None], (lax.axis_size(axis), *value.shape)), axis)


def in_two(value):
    high = value.astype(BF)
    return high, (value - high.astype(F32)).astype(BF)


def dot(a, b, dims=((1,), (0,))):
    return lax.dot_general(a, b, (dims, ((), ())), preferred_element_type=F32)


def body(
    waiting_batchlets,
    arriving_batchlet,
    entry_rescale_factor,
    entry_projection_matrix,
    timescale_projection,
    timescale_offset,
    channel_forgetting_rate,
    state_read_write_matrix,
    direct_passthrough,
    closing_rescale_factor,
    closing_projection_matrix,
):
    gain = entry_rescale_factor[0]
    w_inp = entry_projection_matrix[0]
    w_step = timescale_projection[0]
    bias = timescale_offset[0]
    rates = 0.0005 * jnp.exp2(channel_forgetting_rate[0].astype(F32))
    w_shared = state_read_write_matrix[0]
    skip_coef = direct_passthrough[0]
    o_gain = closing_rescale_factor[0]
    w_outp = closing_projection_matrix[0]

    hi = lax.axis_size("tp_hi")
    lo = lax.axis_size("tp_lo")
    pieces = lax.axis_size(SEQ)
    chips = lax.axis_size("seq_0")
    chip = lax.axis_index("seq_0")
    core = lax.axis_index("seq_1")
    hidden = w_inp.shape[0]
    heads = bias.shape[0]
    channels = heads * HEAD_DIM
    group_size = channels * lo
    here = w_shared.shape[1]
    per = here // hi

    rows = hidden // pieces
    strip = lax.dynamic_slice_in_dim(w_shared, lax.axis_index(SEQ) * rows, rows, 0)
    strip = strip.T.reshape(per, hi, rows).transpose(1, 0, 2)
    own = swap(strip, "tp_hi").reshape(here, rows)
    w_bc = spread(own, SEQ).transpose(1, 0, 2).reshape(here, hidden)

    def mixer(resid):
        count = resid.shape[0]
        far = spread(resid, "tp_hi")
        near = spread(far, "tp_lo")
        values = near.transpose(2, 1, 0, 3).reshape(count, hidden).astype(F32)
        scaled = (values * gain[None, :]).astype(BF)
        inv = lax.rsqrt(jnp.sum(values * values, axis=1, keepdims=True) / hidden + 1e-05)
        share = (dot(scaled, w_bc, ((1,), (1,))) * inv).astype(BF)
        step = jax.nn.softplus(dot(scaled, w_step) * inv + bias[None, :])
        pairs = (dot(scaled, w_inp) * inv).reshape(count, heads, 2, HEAD_DIM)
        xs = pairs[:, :, 0, :]
        gates = pairs[:, :, 1, :]

        cum = jnp.cumsum(-(step * rates[None, :]), axis=0)
        total = cum[count - 1]
        totals = spread(jnp.broadcast_to(total[:, None], (heads, 128)), SEQ)[:, :, 0]

        shared = spread(share, "tp_lo")
        half = here // 2
        bmat = shared[:, :, :half].transpose(1, 0, 2).reshape(count, lo * half)
        cmat = shared[:, :, half:].transpose(1, 0, 2).reshape(count, lo * half)

        xdt = xs * step[:, :, None]
        tail = jnp.exp(total[None, :] - cum)
        pushed = (xdt * tail[:, :, None]).reshape(count, channels).astype(BF)
        local = dot(bmat, pushed, ((0,), (0,)))
        states = spread(local.astype(BF), "seq_0").astype(F32)

        edges = jnp.cumsum(totals, axis=0)
        first = lax.dynamic_index_in_dim(edges - totals, 2 * chip, 0, keepdims=True)
        reach = jnp.where(
            jnp.arange(pieces)[:, None] < 2 * chip, jnp.exp(jnp.minimum(first - edges, 0.0)), 0.0
        )
        mine = lax.dynamic_index_in_dim(reach.reshape(chips, 2, heads), core, 1, keepdims=False)
        mine = jnp.repeat(mine, HEAD_DIM, axis=1)
        before = jnp.sum(states * mine[:, None, :], axis=0)
        across = jnp.exp(lax.dynamic_index_in_dim(totals, 2 * chip, 0, keepdims=True))
        across = jnp.repeat(across, HEAD_DIM, axis=1)
        sent = jnp.where(core == 0, before * across + local, before)
        other = lax.ppermute(sent.astype(BF), "seq_1", [(0, 1), (1, 0)]).astype(F32)
        entering = jnp.where(core == 0, before, before * across) + other

        scores = dot(cmat, bmat, ((1,), (1,)))
        lower = jnp.arange(count)[:, None] >= jnp.arange(count)[None, :]
        decay = jnp.where(
            lower[None], jnp.exp(jnp.minimum(cum.T[:, :, None] - cum.T[:, None, :], 0.0)), 0.0
        )
        intra = jnp.einsum(
            "hts,shp->thp",
            (decay * scores[None]).astype(BF),
            xdt.astype(BF),
            preferred_element_type=F32,
        )
        inter = dot(cmat, entering.astype(BF)).reshape(count, heads, HEAD_DIM)
        inter = inter * jnp.exp(cum)[:, :, None]
        mixed = intra + inter + skip_coef[None, :, None] * xs
        gated = (mixed * jax.nn.silu(gates)).reshape(count, channels)
        part = jnp.sum(gated * gated, axis=1)
        normed = (gated * o_gain[None, :]).astype(BF)
        shares = dot(normed, w_outp).astype(BF)
        shares = shares.reshape(count, hi, lo, -1).transpose(2, 1, 0, 3)
        width = shares.shape[-1]
        shares = shares.reshape(lo, hi * count, width)
        notes = jnp.pad(jnp.stack(in_two(part)), ((0, 14), (0, 0)))
        notes = jnp.broadcast_to(notes[None], (lo, *notes.shape))
        got = swap(jnp.concatenate([shares, notes], axis=1), "tp_lo")
        square = jnp.sum(got[:, hi * count : hi * count + 2].astype(F32), axis=(0, 1))
        unit = lax.rsqrt(square / group_size + 1e-05)
        summed = jnp.sum(got[:, : hi * count].astype(F32), axis=0).reshape(hi, count, width)
        summed = (summed * unit[None, :, None]).astype(BF)
        summed = jnp.sum(swap(summed, "tp_hi").astype(F32), axis=0)
        return (resid.astype(F32) + summed).astype(BF)

    opening = mixer(waiting_batchlets[0])
    sections = lax.axis_size("section")
    moved = lax.ppermute(opening, "section", [(i, i + 1) for i in range(sections - 1)])
    second_in = jnp.where(lax.axis_index("section") == 0, arriving_batchlet, moved)
    return mixer(second_in)[None]


def solution(mesh, cut=None):
    sections, seq, tp = (mesh.shape[name] for name in ("section", "seq", "tp"))
    near = cut or 4
    torus = Mesh(
        mesh.devices.reshape(sections, seq // 2, 2, tp // near, near),
        ("section", *SEQ, *TP),
    )
    return jax.shard_map(
        body,
        mesh=torus,
        in_specs=(
            P("section", SEQ, TP),
            P(SEQ, TP),
            P("section", None),
            P("section", None, TP),
            P("section", None, TP),
            P("section", TP),
            P("section", TP),
            P("section", None, TP),
            P("section", TP),
            P("section", TP),
            P("section", TP, None),
        ),
        out_specs=P("section", SEQ, TP),
        check_vma=False,
    )
```

```python
import jax
import jax.numpy as jnp
from jax import lax
from jax.sharding import Mesh
from jax.sharding import PartitionSpec as P

HEAD_DIM = 64
SEQ = ("seq_0", "seq_1")
TP = ("tp_hi", "tp_lo")
BF = jnp.bfloat16
F32 = jnp.float32


def swap(value, axis):
    return lax.all_to_all(value, axis, 0, 0, tiled=True)


def spread(value, axis):
    return swap(jnp.broadcast_to(value[None], (lax.axis_size(axis), *value.shape)), axis)


def shifted(value, distance):
    size = lax.axis_size(TP)
    return lax.ppermute(value, TP, [(i, (i + distance) % size) for i in range(size)])


def in_two(value):
    high = value.astype(BF)
    return high, (value - high.astype(F32)).astype(BF)


def dot(a, b, dims=((1,), (0,))):
    return lax.dot_general(a, b, (dims, ((), ())), preferred_element_type=F32)


def body(
    waiting_batchlets,
    arriving_batchlet,
    entry_rescale_factor,
    entry_projection_matrix,
    timescale_projection,
    timescale_offset,
    channel_forgetting_rate,
    state_read_write_matrix,
    direct_passthrough,
    closing_rescale_factor,
    closing_projection_matrix,
):
    gain = entry_rescale_factor[0]
    w_inp = entry_projection_matrix[0]
    w_step = timescale_projection[0]
    bias = timescale_offset[0]
    rates = 0.0005 * jnp.exp2(channel_forgetting_rate[0].astype(F32))
    w_shared = state_read_write_matrix[0]
    skip_coef = direct_passthrough[0]
    o_gain = closing_rescale_factor[0]
    w_outp = closing_projection_matrix[0]

    hi = lax.axis_size("tp_hi")
    lo = lax.axis_size("tp_lo")
    pieces = lax.axis_size(SEQ)
    chips = lax.axis_size("seq_0")
    chip = lax.axis_index("seq_0")
    core = lax.axis_index("seq_1")
    hidden = w_inp.shape[0]
    heads = bias.shape[0]
    channels = heads * HEAD_DIM
    group_size = channels * lo
    here = w_shared.shape[1]
    per = here // hi

    rows = hidden // pieces
    strip = lax.dynamic_slice_in_dim(w_shared, lax.axis_index(SEQ) * rows, rows, 0)
    strip = strip.T.reshape(per, hi, rows // 128, 128).transpose(1, 2, 0, 3)
    strip = strip.reshape(hi, rows // 128 * per, 128)
    lo_rank = lax.axis_index("tp_lo")

    def all_columns(own):
        same = spread(own, "seq_0")
        other = lax.ppermute(same, "seq_1", [(0, 1), (1, 0)])
        first = jnp.where(core == 0, same, other)
        second = jnp.where(core == 0, other, same)
        both = jnp.stack([first, second], axis=1)
        both = both.reshape(chips, 2, hi, rows // 128, per, 128).transpose(2, 4, 0, 1, 3, 5)
        return both.reshape(here, hidden)

    def from_near(far):
        half = far.shape[1] // 2
        after = shifted(far, 1)
        ahead = shifted(far, -1)
        opposite = jnp.concatenate([shifted(far[:, :half], 2), shifted(far[:, half:], -2)], axis=1)
        turn = jnp.stack([far, ahead, opposite, after] * 2)
        return lax.dynamic_slice_in_dim(turn, (lo - lo_rank) % lo, lo, 0)

    def mixer(resid, w_bc):
        count = resid.shape[0]
        sent = jnp.broadcast_to(resid[None], (hi, *resid.shape))
        if w_bc is None:
            got = swap(jnp.concatenate([sent, strip], axis=1), "tp_hi")
            far = got[:, :count]
            w_bc = all_columns(got[:, count:])
        else:
            far = swap(sent, "tp_hi")
        near = from_near(far)
        values = near.transpose(2, 1, 0, 3).reshape(count, hidden).astype(F32)
        scaled = (values * gain[None, :]).astype(BF)
        inv = lax.rsqrt(jnp.sum(values * values, axis=1, keepdims=True) / hidden + 1e-05)
        share = (dot(scaled, w_bc, ((1,), (1,))) * inv).astype(BF)
        step = jax.nn.softplus(dot(scaled, w_step) * inv + bias[None, :])
        pairs = (dot(scaled, w_inp) * inv).reshape(count, heads, 2, HEAD_DIM)
        xs = pairs[:, :, 0, :]
        gates = pairs[:, :, 1, :]

        cum = jnp.cumsum(-(step * rates[None, :]), axis=0)
        total = cum[count - 1]
        twin = lax.ppermute(jnp.broadcast_to(total[None], (8, heads)), "seq_1", [(0, 1), (1, 0)])[0]
        pair = jnp.where(core == 0, jnp.stack([total, twin]), jnp.stack([twin, total]))
        notes = jnp.repeat(jnp.concatenate(in_two(pair)), HEAD_DIM, axis=1)
        notes = jnp.pad(notes, ((0, 12), (0, 0)))

        shared = spread(share, "tp_lo")
        half = here // 2
        bmat = shared[:, :, :half].transpose(1, 0, 2).reshape(count, lo * half)
        cmat = shared[:, :, half:].transpose(1, 0, 2).reshape(count, lo * half)

        xdt = xs * step[:, :, None]
        tail = jnp.exp(total[None, :] - cum)
        pushed = (xdt * tail[:, :, None]).reshape(count, channels).astype(BF)
        local = dot(bmat, pushed, ((0,), (0,)))
        got = spread(jnp.concatenate([local.astype(BF), notes]), "seq_0").astype(F32)
        depth = local.shape[0]
        states = got[:, :depth]
        totals = (got[:, depth : depth + 2] + got[:, depth + 2 : depth + 4]).reshape(pieces, channels)

        edges = jnp.cumsum(totals, axis=0)
        first = lax.dynamic_index_in_dim(edges - totals, 2 * chip, 0, keepdims=True)
        reach = jnp.where(
            jnp.arange(pieces)[:, None] < 2 * chip, jnp.exp(jnp.minimum(first - edges, 0.0)), 0.0
        )
        mine = lax.dynamic_index_in_dim(reach.reshape(chips, 2, channels), core, 1, keepdims=False)
        before = jnp.sum(states * mine[:, None, :], axis=0)
        across = jnp.exp(lax.dynamic_index_in_dim(totals, 2 * chip, 0, keepdims=True))
        sent = jnp.where(core == 0, before * across + local, before)
        other = lax.ppermute(sent.astype(BF), "seq_1", [(0, 1), (1, 0)]).astype(F32)
        entering = jnp.where(core == 0, before, before * across) + other

        scores = dot(cmat, bmat, ((1,), (1,)))
        lower = jnp.arange(count)[:, None] >= jnp.arange(count)[None, :]
        decay = jnp.where(
            lower[None], jnp.exp(jnp.minimum(cum.T[:, :, None] - cum.T[:, None, :], 0.0)), 0.0
        )
        intra = jnp.einsum(
            "hts,shp->thp",
            (decay * scores[None]).astype(BF),
            xdt.astype(BF),
            preferred_element_type=F32,
        )
        inter = dot(cmat, entering.astype(BF)).reshape(count, heads, HEAD_DIM)
        inter = inter * jnp.exp(cum)[:, :, None]
        mixed = intra + inter + skip_coef[None, :, None] * xs
        gated = (mixed * jax.nn.silu(gates)).reshape(count, channels)
        part = jnp.sum(gated * gated, axis=1)
        normed = (gated * o_gain[None, :]).astype(BF)
        shares = dot(normed, w_outp).astype(BF)
        shares = shares.reshape(count, hi, lo, -1).transpose(2, 1, 0, 3)
        width = shares.shape[-1]
        shares = shares.reshape(lo, hi * count, width)
        notes = jnp.pad(jnp.stack(in_two(part)), ((0, 14), (0, 0)))
        notes = jnp.broadcast_to(notes[None], (lo, *notes.shape))
        got = swap(jnp.concatenate([shares, notes], axis=1), "tp_lo")
        square = jnp.sum(got[:, hi * count : hi * count + 2].astype(F32), axis=(0, 1))
        unit = lax.rsqrt(square / group_size + 1e-05)
        summed = jnp.sum(got[:, : hi * count].astype(F32), axis=0).reshape(hi, count, width)
        summed = (summed * unit[None, :, None]).astype(BF)
        summed = jnp.sum(swap(summed, "tp_hi").astype(F32), axis=0)
        return (resid.astype(F32) + summed).astype(BF), w_bc

    opening, w_bc = mixer(waiting_batchlets[0], None)
    sections = lax.axis_size("section")
    moved = lax.ppermute(opening, "section", [(i, i + 1) for i in range(sections - 1)])
    second_in = jnp.where(lax.axis_index("section") == 0, arriving_batchlet, moved)
    return mixer(second_in, w_bc)[0][None]


def solution(mesh, cut=None):
    sections, seq, tp = (mesh.shape[name] for name in ("section", "seq", "tp"))
    near = cut or 4
    torus = Mesh(
        mesh.devices.reshape(sections, seq // 2, 2, tp // near, near),
        ("section", *SEQ, *TP),
    )
    return jax.shard_map(
        body,
        mesh=torus,
        in_specs=(
            P("section", SEQ, TP),
            P(SEQ, TP),
            P("section", None),
            P("section", None, TP),
            P("section", None, TP),
            P("section", TP),
            P("section", TP),
            P("section", None, TP),
            P("section", TP),
            P("section", TP),
            P("section", TP, None),
        ),
        out_specs=P("section", SEQ, TP),
        check_vma=False,
    )
```

```python
import jax
import jax.numpy as jnp
from jax import lax
from jax.experimental import pallas as pl
from jax.experimental.pallas import tpu as pltpu
from jax.sharding import Mesh
from jax.sharding import PartitionSpec as P

HEAD_DIM = 64
SEQ = ("seq_0", "seq_1")
TP = ("tp_hi", "tp_lo")
BF = jnp.bfloat16
F32 = jnp.float32
EXACT = lax.Precision.HIGHEST
INTERPRET = False


def swap(value, axis):
    return lax.all_to_all(value, axis, 0, 0, tiled=True)


def spread(value, axis):
    return swap(jnp.broadcast_to(value[None], (lax.axis_size(axis), *value.shape)), axis)


def shifted(value, distance):
    size = lax.axis_size(TP)
    return lax.ppermute(value, TP, [(i, (i + distance) % size) for i in range(size)])


def dot(a, b, dims=((1,), (0,))):
    return lax.dot_general(a, b, (dims, ((), ())), preferred_element_type=F32)


def lanes_of(value):
    low = lax.broadcasted_iota(jnp.int32, (value.shape[0], 128), 1) < HEAD_DIM
    return jnp.concatenate(
        [jnp.where(low, value[:, h : h + 1], value[:, h + 1 : h + 2]) for h in (0, 2)], axis=1
    )


def split_pair(a, b):
    low = lax.broadcasted_iota(jnp.int32, a.shape, 1) < 64
    first = jnp.where(low, a, pltpu.roll(b, 64, 1))
    second = jnp.where(low, pltpu.roll(a, 64, 1), b)
    return first, second


def project_kernel(
    place, far, ahead, across_a, across_b, behind, gain, w_inp, same, other, w_step, bias, rates,
    share, x_out, g_out, step_out, cum_out, total_out, order, acc_p, acc_b, acc_s, acc_q,
):
    i = pl.program_id(0)
    lo = order.shape[0]
    me = place[0]
    core = place[1]
    count = order.shape[1]
    half = count // 2

    @pl.when(i == 0)
    def _():
        acc_p[...] = jnp.zeros_like(acc_p)
        acc_b[...] = jnp.zeros_like(acc_b)
        acc_s[...] = jnp.zeros_like(acc_s)
        acc_q[...] = jnp.zeros_like(acc_q)

    order[me] = far[0]
    order[(me + 1) % lo] = ahead[0]
    order[(me + 2) % lo, :half] = across_a[0]
    order[(me + 2) % lo, half:] = across_b[0]
    order[(me + 3) % lo] = behind[0]
    values = jnp.concatenate([order[j] for j in range(lo)], axis=1).astype(F32)
    row = jnp.concatenate([gain[0, j : j + 1] for j in range(lo)], axis=1)
    acc_q[...] += jnp.sum(values * values, axis=1, keepdims=True)
    scaled = (values * row).astype(BF)
    acc_p[...] += dot(scaled, w_inp[...])
    acc_s[...] += dot(scaled, w_step[...])

    def add_share(ref):
        parts = [ref[0, :, j].reshape(128, 128) for j in range(lo)]
        acc_b[...] += dot(scaled, jnp.concatenate(parts, axis=1), ((1,), (1,)))

    @pl.when(i % 2 == core)
    def _():
        add_share(same)

    @pl.when(i % 2 != core)
    def _():
        add_share(other)

    @pl.when(i == pl.num_programs(0) - 1)
    def _():
        inv = lax.rsqrt(acc_q[...] / w_total(w_inp, i) + 1e-05)
        sent = (acc_b[...] * inv).astype(BF)
        for j in range(lo):
            share[j] = sent
        for q in (0, 1):
            left = acc_p[:, 256 * q : 256 * q + 128] * inv
            right = acc_p[:, 256 * q + 128 : 256 * q + 256] * inv
            xs, gates = split_pair(left, right)
            x_out[:, 128 * q : 128 * q + 128] = xs
            g_out[:, 128 * q : 128 * q + 128] = gates
        raw = acc_s[...] * inv + bias[...]
        step = jnp.maximum(raw, 0.0) + jnp.log1p(jnp.exp(-jnp.abs(raw)))
        step_out[...] = step
        shape = (count, count)
        lower = lax.broadcasted_iota(jnp.int32, shape, 0) >= lax.broadcasted_iota(jnp.int32, shape, 1)
        cum = jnp.dot(
            lower.astype(F32), -(step * rates[...]), precision=EXACT, preferred_element_type=F32
        )
        cum_out[...] = cum
        total_out[...] = jnp.broadcast_to(cum[count - 1 : count], total_out.shape)


def w_total(w_inp, i):
    return w_inp.shape[0] * pl.num_programs(0)


def piece_kernel(
    place, shared, x_in, step, cum, twin, skip, sent, local, y_out, c_out, grow
):
    core = place[1]
    count = x_in.shape[0]
    pairs = [
        split_pair(shared[k].astype(F32), shared[k + 1].astype(F32))
        for k in range(0, shared.shape[0], 2)
    ]
    bmat = jnp.concatenate([p[0] for p in pairs], axis=1).astype(BF)
    cmat = jnp.concatenate([p[1] for p in pairs], axis=1).astype(BF)
    c_out[...] = cmat
    scores = dot(cmat, bmat, ((1,), (1,)))
    cums = cum[...]
    turned = cums.T
    xs = x_in[...]
    xdt = xs * lanes_of(step[...])
    total = cums[count - 1 : count]
    pushed = (xdt * lanes_of(jnp.exp(total - cums))).astype(BF)
    states = dot(bmat, pushed, ((0,), (0,)))
    local[...] = states
    xdt = xdt.astype(BF)
    shape = (count, count)
    lower = lax.broadcasted_iota(jnp.int32, shape, 0) >= lax.broadcasted_iota(jnp.int32, shape, 1)
    low = lax.broadcasted_iota(jnp.int32, (count, 128), 1) < HEAD_DIM
    for q in (0, 1):
        block = xdt[:, 128 * q : 128 * q + 128]
        made = []
        for h in (2 * q, 2 * q + 1):
            gap = jnp.minimum(cums[:, h : h + 1] - turned[h : h + 1, :], 0.0)
            mask = jnp.where(lower, jnp.exp(gap), 0.0) * scores
            made.append(dot(mask.astype(BF), block))
        at = slice(128 * q, 128 * q + 128)
        y_out[:, at] = jnp.where(low, made[0], made[1]) + skip[:, at] * xs[:, at]
    grow[...] = lanes_of(jnp.exp(cums))
    mine = lanes_of(total)
    theirs = lanes_of(twin[0:1])
    first = jnp.where(core == 0, mine, theirs)
    second = jnp.where(core == 0, theirs, mine)
    line = lax.broadcasted_iota(jnp.int32, (16, first.shape[1]), 0)
    high_a = first.astype(BF).astype(F32)
    high_b = second.astype(BF).astype(F32)
    notes = jnp.where(line == 0, high_a, 0.0)
    notes = jnp.where(line == 1, high_b, notes)
    notes = jnp.where(line == 2, first - high_a, notes)
    notes = jnp.where(line == 3, second - high_b, notes).astype(BF)
    depth = states.shape[0]
    states = states.astype(BF)
    for k in range(sent.shape[0]):
        sent[k, :depth] = states
        sent[k, depth:] = notes


def carry_kernel(place, got, local, sent, keep):
    core = place[1]
    chip = place[2]
    chips = got.shape[0]
    depth = local.shape[0]
    firsts, seconds = [], []
    for k in range(chips):
        notes = got[k, depth:].astype(F32)
        firsts.append(notes[0:1] + notes[2:3])
        seconds.append(notes[1:2] + notes[3:4])
    until = jnp.zeros_like(firsts[0])
    own = jnp.zeros_like(firsts[0])
    for k in range(chips):
        until = until + jnp.where(k < chip, firsts[k] + seconds[k], 0.0)
        own = own + jnp.where(k == chip, firsts[k], 0.0)
    before = jnp.zeros(local.shape, F32)
    edge = jnp.zeros_like(firsts[0])
    for k in range(chips - 1):
        end = edge + firsts[k] + jnp.where(core == 1, seconds[k], 0.0)
        weight = jnp.where(k < chip, jnp.exp(jnp.minimum(until - end, 0.0)), 0.0)
        before = before + weight * got[k, :depth].astype(F32)
        edge = edge + firsts[k] + seconds[k]
    moved = before * jnp.exp(own)
    sent[...] = jnp.where(core == 0, moved + local[...], before).astype(BF)
    keep[...] = jnp.where(core == 0, before, moved)


def gate_kernel(other, keep, cmat, y_in, grow, g_in, o_gain, sent):
    entering = (keep[...] + other[...].astype(F32)).astype(BF)
    mixed = y_in[...] + dot(cmat[...], entering) * grow[...]
    gates = g_in[...]
    gated = mixed * (gates * lax.logistic(gates))
    squares = gated * gated
    count, width = squares.shape
    part = lax.dot_general(
        jnp.ones((16, width), F32),
        squares,
        (((1,), (1,)), ((), ())),
        precision=EXACT,
        preferred_element_type=F32,
    )
    high = part.astype(BF).astype(F32)
    line = lax.broadcasted_iota(jnp.int32, part.shape, 0)
    notes = jnp.where(line == 0, high, jnp.where(line == 1, part - high, 0.0))
    notes = jnp.concatenate([notes, jnp.zeros((16, width - count), F32)], axis=1).astype(BF)
    out = (gated * o_gain[...]).astype(BF)
    for k in range(sent.shape[0]):
        sent[k, :count] = out
        sent[k, count:] = notes


def close_kernel(got, weight, sent):
    lo = got.shape[0]
    count = sent.shape[1]
    left = jnp.concatenate([got[k, :count] for k in range(lo)], axis=1)
    product = dot(left, weight[...])
    square = jnp.zeros((16, count), F32)
    for k in range(lo):
        square = square + got[k, count:, :count].astype(F32)
    unit = lax.rsqrt((square[0:1] + square[1:2]) / left.shape[1] + 1e-05)
    shape = (count, count)
    same = lax.broadcasted_iota(jnp.int32, shape, 0) == lax.broadcasted_iota(jnp.int32, shape, 1)
    unit = jnp.sum(jnp.where(same, unit, 0.0), axis=1, keepdims=True)
    product = (product * unit).astype(BF)
    for k in range(sent.shape[0]):
        sent[k] = product[:, 128 * k : 128 * k + 128]


SCALARS = pl.BlockSpec(memory_space=pltpu.SMEM)


def whole(shape):
    return pl.BlockSpec(shape, lambda *_: (0,) * len(shape))


def run(kernel, name, args, outs, place=None):
    specs = [whole(a.shape) for a in args]
    if place is not None:
        args, specs = (place, *args), [SCALARS, *specs]
    return pl.pallas_call(
        kernel,
        out_shape=[jax.ShapeDtypeStruct(*o) for o in outs],
        in_specs=specs,
        out_specs=[whole(o[0]) for o in outs],
        interpret=INTERPRET,
        name=name,
    )(*args)


def body(
    waiting_batchlets,
    arriving_batchlet,
    entry_rescale_factor,
    entry_projection_matrix,
    timescale_projection,
    timescale_offset,
    channel_forgetting_rate,
    state_read_write_matrix,
    direct_passthrough,
    closing_rescale_factor,
    closing_projection_matrix,
):
    gain = entry_rescale_factor[0]
    w_inp = entry_projection_matrix[0]
    w_step = timescale_projection[0]
    bias = timescale_offset[0]
    rates = 0.0005 * jnp.exp2(channel_forgetting_rate[0].astype(F32))
    w_shared = state_read_write_matrix[0]
    skip_coef = direct_passthrough[0]
    o_gain = closing_rescale_factor[0]
    w_outp = closing_projection_matrix[0]

    hi = lax.axis_size("tp_hi")
    lo = lax.axis_size("tp_lo")
    pieces = lax.axis_size(SEQ)
    chips = lax.axis_size("seq_0")
    chip = lax.axis_index("seq_0")
    core = lax.axis_index("seq_1")
    hidden = w_inp.shape[0]
    heads = bias.shape[0]
    channels = heads * HEAD_DIM
    group_size = channels * lo
    here = w_shared.shape[1]
    per = here // hi

    rows = hidden // pieces
    strip = lax.dynamic_slice_in_dim(w_shared, lax.axis_index(SEQ) * rows, rows, 0)
    strip = strip.T.reshape(per, hi, rows // 128, 128).transpose(1, 2, 0, 3)
    strip = strip.reshape(hi, rows // 128 * per, 128)
    lo_rank = lax.axis_index("tp_lo")

    def both_cores(same):
        other = lax.ppermute(same, "seq_1", [(0, 1), (1, 0)])
        return same, other

    def turned(parts, rank):
        ring = jnp.stack(parts * 2)
        size = len(parts)
        return lax.dynamic_slice_in_dim(ring, (size - rank) % size, size, 0)

    def from_ring(value, axis, pick):
        size = lax.axis_size(axis)
        parts = [pick(value, 0)]
        for k in range(1, size):
            route = [(i, (i - k) % size) for i in range(size)]
            parts.append(lax.ppermute(pick(value, -k), axis, route))
        return turned(parts, lax.axis_index(axis))

    strip_rows = channels // pieces
    cut = lax.dynamic_slice_in_dim(w_outp, lax.axis_index(SEQ) * strip_rows, strip_rows, 0)
    cut = cut.reshape(strip_rows, hi, lo, 128).transpose(2, 0, 1, 3).reshape(lo, strip_rows, hi * 128)

    def for_peer(value, k):
        return lax.dynamic_index_in_dim(value, (lo_rank + k) % lo, 0, keepdims=False)

    group_rows = from_ring(cut, "tp_lo", for_peer)
    group_rows = from_ring(group_rows, "seq_0", lambda value, k: value)
    same, other = both_cores(group_rows)
    w_out = jnp.stack([jnp.where(core == 0, same, other), jnp.where(core == 0, other, same)])
    w_out = w_out.transpose(2, 1, 0, 3, 4).reshape(group_size, hi * 128)

    place = jnp.stack([lo_rank, core, chip]).astype(jnp.int32)
    gain = gain.reshape(hi, lo, 128)
    w_step = jnp.pad(w_step, ((0, 0), (0, 128 - heads)))
    bias = jnp.pad(bias, (0, 128 - heads))[None]
    rates = jnp.pad(rates, (0, 128 - heads))[None]
    skip = jnp.repeat(skip_coef, HEAD_DIM)[None]
    o_gain = o_gain[None]

    def mixer(resid, w_bc):
        count = resid.shape[0]
        half = count // 2
        sent = jnp.broadcast_to(resid[None], (hi, *resid.shape))
        if w_bc is None:
            got = swap(jnp.concatenate([sent, strip], axis=1), "tp_hi")
            far = got[:, :count]
            own = got[:, count:].reshape(hi, rows // 128, per, 128)
            w_bc = both_cores(spread(own, "seq_0"))
        else:
            far = swap(sent, "tp_hi")
        behind = shifted(far, 1)
        ahead = shifted(far, -1)
        across_a = shifted(far[:, :half], 2)
        across_b = shifted(far[:, half:], -2)

        def by_hi(rows_here):
            return pl.BlockSpec((1, rows_here, 128), lambda i: (i, 0, 0))

        strip_spec = pl.BlockSpec((1, *w_bc[0].shape[1:]), lambda i: (i // 2, 0, 0, 0, 0))
        tall = lo * 128
        outs = [
            ((lo, count, 128), BF),
            ((count, channels), F32),
            ((count, channels), F32),
            ((count, 128), F32),
            ((count, 128), F32),
            ((8, 128), F32),
        ]
        share, xs, gates, step, cum, total = pl.pallas_call(
            project_kernel,
            grid=(hi,),
            out_shape=[jax.ShapeDtypeStruct(*o) for o in outs],
            in_specs=[
                SCALARS,
                by_hi(count),
                by_hi(count),
                by_hi(half),
                by_hi(half),
                by_hi(count),
                pl.BlockSpec((1, lo, 128), lambda i: (i, 0, 0)),
                pl.BlockSpec((tall, w_inp.shape[1]), lambda i: (i, 0)),
                strip_spec,
                strip_spec,
                pl.BlockSpec((tall, 128), lambda i: (i, 0)),
                whole((1, 128)),
                whole((1, 128)),
            ],
            out_specs=[whole(o[0]) for o in outs],
            scratch_shapes=[
                pltpu.VMEM((lo, count, 128), BF),
                pltpu.VMEM((count, w_inp.shape[1]), F32),
                pltpu.VMEM((count, 128), F32),
                pltpu.VMEM((count, 128), F32),
                pltpu.VMEM((count, 1), F32),
            ],
            interpret=INTERPRET,
            name="project",
        )(place, far, ahead, across_a, across_b, behind, gain, w_inp, *w_bc, w_step, bias, rates)

        twin = lax.ppermute(total, "seq_1", [(0, 1), (1, 0)])
        shared = swap(share, "tp_lo")
        depth = lo * here // 2
        sent, local, y, cmat, grow = run(
            piece_kernel,
            "piece",
            (shared, xs, step, cum, twin, skip),
            [
                ((chips, depth + 16, channels), BF),
                ((depth, channels), F32),
                ((count, channels), F32),
                ((count, depth), BF),
                ((count, channels), F32),
            ],
            place,
        )
        got = swap(sent, "seq_0")
        sent, keep = run(
            carry_kernel,
            "carry",
            (got, local),
            [((depth, channels), BF), ((depth, channels), F32)],
            place,
        )
        other = lax.ppermute(sent, "seq_1", [(0, 1), (1, 0)])
        (sent,) = run(
            gate_kernel,
            "gate",
            (other, keep, cmat, y, grow, gates, o_gain),
            [((lo, count + 16, channels), BF)],
        )
        got = swap(sent, "tp_lo")
        shares = pl.pallas_call(
            close_kernel,
            grid=(hi // 2,),
            out_shape=jax.ShapeDtypeStruct((hi, count, 128), BF),
            in_specs=[
                whole(got.shape),
                pl.BlockSpec((group_size, 256), lambda i: (0, i)),
            ],
            out_specs=pl.BlockSpec((2, count, 128), lambda i: (i, 0, 0)),
            interpret=INTERPRET,
            name="close",
        )(got, w_out)
        summed = jnp.sum(swap(shares, "tp_hi").astype(F32), axis=0)
        return (resid.astype(F32) + summed).astype(BF), w_bc

    opening, w_bc = mixer(waiting_batchlets[0], None)
    sections = lax.axis_size("section")
    moved = lax.ppermute(opening, "section", [(i, i + 1) for i in range(sections - 1)])
    second_in = jnp.where(lax.axis_index("section") == 0, arriving_batchlet, moved)
    return mixer(second_in, w_bc)[0][None]


def solution(mesh, cut=None):
    sections, seq, tp = (mesh.shape[name] for name in ("section", "seq", "tp"))
    near = cut or 4
    torus = Mesh(
        mesh.devices.reshape(sections, seq // 2, 2, tp // near, near),
        ("section", *SEQ, *TP),
    )
    return jax.shard_map(
        body,
        mesh=torus,
        in_specs=(
            P("section", SEQ, TP),
            P(SEQ, TP),
            P("section", None),
            P("section", None, TP),
            P("section", None, TP),
            P("section", TP),
            P("section", TP),
            P("section", None, TP),
            P("section", TP),
            P("section", TP),
            P("section", TP, None),
        ),
        out_specs=P("section", SEQ, TP),
        check_vma=False,
    )
```

```python
import jax
import jax.numpy as jnp
from jax import lax
from jax.experimental import pallas as pl
from jax.experimental.pallas import tpu as pltpu
from jax.sharding import Mesh
from jax.sharding import PartitionSpec as P

HEAD_DIM = 64
SEQ = ("seq_0", "seq_1")
TP = ("tp_hi", "tp_lo")
BF = jnp.bfloat16
F32 = jnp.float32
EXACT = lax.Precision.HIGHEST
INTERPRET = False


def swap(value, axis):
    return lax.all_to_all(value, axis, 0, 0, tiled=True)


def shifted(value, distance):
    size = lax.axis_size(TP)
    return lax.ppermute(value, TP, [(i, (i + distance) % size) for i in range(size)])


def dot(a, b, dims=((1,), (0,))):
    return lax.dot_general(a, b, (dims, ((), ())), preferred_element_type=F32)


def lanes_of(value):
    low = lax.broadcasted_iota(jnp.int32, (value.shape[0], 128), 1) < HEAD_DIM
    return jnp.concatenate(
        [jnp.where(low, value[:, h : h + 1], value[:, h + 1 : h + 2]) for h in (0, 2)], axis=1
    )


def split_pair(a, b):
    low = lax.broadcasted_iota(jnp.int32, a.shape, 1) < 64
    first = jnp.where(low, a, pltpu.roll(b, 64, 1))
    second = jnp.where(low, pltpu.roll(a, 64, 1), b)
    return first, second


def project_kernel(
    place, far, ahead, across_a, across_b, behind, gain, w_inp, same, other, w_step, bias, rates,
    share, x_out, g_out, step_out, cum_out, total_out,
    order, ready, steps, acc_p, acc_b, acc_s, acc_q,
):
    i = pl.program_id(0)
    lo = order.shape[1]
    me = place[0]
    core = place[1]
    count = order.shape[2]
    half = count // 2
    tall = lo * 128

    @pl.when(i == 0)
    def _():
        acc_p[...] = jnp.zeros_like(acc_p)
        acc_b[...] = jnp.zeros_like(acc_b)
        acc_s[...] = jnp.zeros_like(acc_s)
        acc_q[...] = jnp.zeros_like(acc_q)
        steps[...] = jnp.zeros_like(steps)

    for u in (0, 1):
        order[u, me] = far[u]
        order[u, (me + 1) % lo] = ahead[u]
        order[u, (me + 2) % lo, :half] = across_a[u]
        order[u, (me + 2) % lo, half:] = across_b[u]
        order[u, (me + 3) % lo] = behind[u]
        values = jnp.concatenate([order[u, j] for j in range(lo)], axis=1).astype(F32)
        row = jnp.concatenate([gain[u, j : j + 1] for j in range(lo)], axis=1)
        acc_q[...] += jnp.sum(values * values, axis=1, keepdims=True)
        ready[u] = (values * row).astype(BF)

    scaled = jnp.concatenate([ready[0], ready[1]], axis=1)
    steps[:16] = w_step[...]
    acc_p[...] += dot(scaled, w_inp[...])
    acc_s[...] += dot(scaled, steps[...], ((1,), (1,)))
    for ref, source in ((same, core), (other, 1 - core)):
        parts = [ref[0, :, j].reshape(128, 128) for j in range(lo)]
        acc_b[...] += dot(ready[source], jnp.concatenate(parts, axis=1), ((1,), (1,)))

    @pl.when(i == pl.num_programs(0) - 1)
    def _():
        inv = lax.rsqrt(acc_q[...] / (2 * tall * pl.num_programs(0)) + 1e-05)
        sent = (acc_b[...] * inv).astype(BF)
        for j in range(lo):
            share[j] = sent
        for q in (0, 1):
            left = acc_p[:, 256 * q : 256 * q + 128] * inv
            right = acc_p[:, 256 * q + 128 : 256 * q + 256] * inv
            xs, gates = split_pair(left, right)
            x_out[:, 128 * q : 128 * q + 128] = xs
            g_out[:, 128 * q : 128 * q + 128] = gates
        raw = acc_s[...] * inv + bias[...]
        step = jnp.maximum(raw, 0.0) + jnp.log1p(jnp.exp(-jnp.abs(raw)))
        step_out[...] = step
        shape = (count, count)
        lower = lax.broadcasted_iota(jnp.int32, shape, 0) >= lax.broadcasted_iota(jnp.int32, shape, 1)
        cum = jnp.dot(
            lower.astype(F32), -(step * rates[...]), precision=EXACT, preferred_element_type=F32
        )
        cum_out[...] = cum
        total_out[...] = jnp.broadcast_to(cum[count - 1 : count], total_out.shape)


def piece_kernel(
    place, shared, x_in, step, cum, twin, skip, sent, local, y_out, c_out, grow
):
    core = place[1]
    count = x_in.shape[0]
    pairs = [
        split_pair(shared[k].astype(F32), shared[k + 1].astype(F32))
        for k in range(0, shared.shape[0], 2)
    ]
    bmat = jnp.concatenate([p[0] for p in pairs], axis=1).astype(BF)
    cmat = jnp.concatenate([p[1] for p in pairs], axis=1).astype(BF)
    c_out[...] = cmat
    scores = dot(cmat, bmat, ((1,), (1,)))
    cums = cum[...]
    turned = cums.T
    xs = x_in[...]
    xdt = xs * lanes_of(step[...])
    total = cums[count - 1 : count]
    pushed = (xdt * lanes_of(jnp.exp(total - cums))).astype(BF)
    states = dot(bmat, pushed, ((0,), (0,)))
    local[...] = states
    xdt = xdt.astype(BF)
    shape = (count, count)
    lower = lax.broadcasted_iota(jnp.int32, shape, 0) >= lax.broadcasted_iota(jnp.int32, shape, 1)
    low = lax.broadcasted_iota(jnp.int32, (count, 128), 1) < HEAD_DIM
    for q in (0, 1):
        block = xdt[:, 128 * q : 128 * q + 128]
        made = []
        for h in (2 * q, 2 * q + 1):
            gap = jnp.minimum(cums[:, h : h + 1] - turned[h : h + 1, :], 0.0)
            mask = jnp.where(lower, jnp.exp(gap), 0.0) * scores
            made.append(dot(mask.astype(BF), block))
        at = slice(128 * q, 128 * q + 128)
        y_out[:, at] = jnp.where(low, made[0], made[1]) + skip[:, at] * xs[:, at]
    grow[...] = lanes_of(jnp.exp(cums))
    mine = lanes_of(total)
    theirs = lanes_of(twin[0:1])
    first = jnp.where(core == 0, mine, theirs)
    second = jnp.where(core == 0, theirs, mine)
    line = lax.broadcasted_iota(jnp.int32, (16, first.shape[1]), 0)
    high_a = first.astype(BF).astype(F32)
    high_b = second.astype(BF).astype(F32)
    notes = jnp.where(line == 0, high_a, 0.0)
    notes = jnp.where(line == 1, high_b, notes)
    notes = jnp.where(line == 2, first - high_a, notes)
    notes = jnp.where(line == 3, second - high_b, notes).astype(BF)
    depth = states.shape[0]
    states = states.astype(BF)
    for k in range(sent.shape[0]):
        sent[k, :depth] = states
        sent[k, depth:] = notes


def carry_kernel(place, got, local, sent, keep):
    core = place[1]
    chip = place[2]
    chips = got.shape[0]
    depth = local.shape[0]
    firsts, seconds = [], []
    for k in range(chips):
        notes = got[k, depth:].astype(F32)
        firsts.append(notes[0:1] + notes[2:3])
        seconds.append(notes[1:2] + notes[3:4])
    until = jnp.zeros_like(firsts[0])
    own = jnp.zeros_like(firsts[0])
    for k in range(chips):
        until = until + jnp.where(k < chip, firsts[k] + seconds[k], 0.0)
        own = own + jnp.where(k == chip, firsts[k], 0.0)
    before = jnp.zeros(local.shape, F32)
    edge = jnp.zeros_like(firsts[0])
    for k in range(chips - 1):
        end = edge + firsts[k] + jnp.where(core == 1, seconds[k], 0.0)
        weight = jnp.where(k < chip, jnp.exp(jnp.minimum(until - end, 0.0)), 0.0)
        before = before + weight * got[k, :depth].astype(F32)
        edge = edge + firsts[k] + seconds[k]
    moved = before * jnp.exp(own)
    sent[...] = jnp.where(core == 0, moved + local[...], before).astype(BF)
    keep[...] = jnp.where(core == 0, before, moved)


def gate_kernel(other, keep, cmat, y_in, grow, g_in, o_gain, sent):
    entering = (keep[...] + other[...].astype(F32)).astype(BF)
    mixed = y_in[...] + dot(cmat[...], entering) * grow[...]
    gates = g_in[...]
    gated = mixed * (gates * lax.logistic(gates))
    squares = gated * gated
    count, width = squares.shape
    part = lax.dot_general(
        jnp.ones((16, width), F32),
        squares,
        (((1,), (1,)), ((), ())),
        precision=EXACT,
        preferred_element_type=F32,
    )
    high = part.astype(BF).astype(F32)
    line = lax.broadcasted_iota(jnp.int32, part.shape, 0)
    notes = jnp.where(line == 0, high, jnp.where(line == 1, part - high, 0.0))
    notes = jnp.concatenate([notes, jnp.zeros((16, width - count), F32)], axis=1).astype(BF)
    out = (gated * o_gain[...]).astype(BF)
    for k in range(sent.shape[0]):
        sent[k, :count] = out
        sent[k, count:] = notes


def close_kernel(place, got, same, other, sent):
    lo = got.shape[0]
    count = sent.shape[1]
    chips = pl.num_programs(0)
    order = [(place[0] + lo - k) % lo for k in range(lo)]
    left = jnp.concatenate([got[k, :count] for k in order], axis=1)
    square = jnp.zeros((16, count), F32)
    for k in range(lo):
        square = square + got[k, count:, :count].astype(F32)
    unit = lax.rsqrt((square[0:1] + square[1:2]) / left.shape[1] + 1e-05)
    shape = (count, count)
    diagonal = lax.broadcasted_iota(jnp.int32, shape, 0) == lax.broadcasted_iota(jnp.int32, shape, 1)
    unit = jnp.sum(jnp.where(diagonal, unit, 0.0), axis=1, keepdims=True)
    height = left.shape[1]
    weight = [ref[0].reshape(height, 128) for ref in (same, other)]
    product = (dot(left, jnp.concatenate(weight, axis=1)) * unit).astype(BF)
    start = 2 * ((place[2] + pl.program_id(0)) % chips)
    sent[start + place[1]] = product[:, :128]
    sent[start + 1 - place[1]] = product[:, 128:]


SCALARS = pl.BlockSpec(memory_space=pltpu.SMEM)


def whole(shape):
    return pl.BlockSpec(shape, lambda *_: (0,) * len(shape))


def run(kernel, args, outs, place=None):
    local = pl.BlockSpec(memory_space=pltpu.VMEM)
    specs = [local for _ in args]
    if place is not None:
        args, specs = (place, *args), [SCALARS, *specs]
    return pl.pallas_call(
        kernel,
        out_shape=[jax.ShapeDtypeStruct(*o) for o in outs],
        in_specs=specs,
        out_specs=[local for _ in outs],
        interpret=INTERPRET,
    )(*args)


def body(
    waiting_batchlets,
    arriving_batchlet,
    entry_rescale_factor,
    entry_projection_matrix,
    timescale_projection,
    timescale_offset,
    channel_forgetting_rate,
    state_read_write_matrix,
    direct_passthrough,
    closing_rescale_factor,
    closing_projection_matrix,
):
    gain = entry_rescale_factor[0]
    w_inp = entry_projection_matrix[0]
    w_step = timescale_projection[0]
    bias = timescale_offset[0]
    rates = 0.0005 * jnp.exp2(channel_forgetting_rate[0].astype(F32))
    w_shared = state_read_write_matrix[0]
    skip_coef = direct_passthrough[0]
    o_gain = closing_rescale_factor[0]
    w_outp = closing_projection_matrix[0]

    hi = lax.axis_size("tp_hi")
    lo = lax.axis_size("tp_lo")
    pieces = lax.axis_size(SEQ)
    chips = lax.axis_size("seq_0")
    chip = lax.axis_index("seq_0")
    core = lax.axis_index("seq_1")
    hidden = w_inp.shape[0]
    heads = bias.shape[0]
    channels = heads * HEAD_DIM
    here = w_shared.shape[1]
    per = here // hi

    rows = hidden // pieces
    strip = lax.dynamic_slice_in_dim(w_shared, lax.axis_index(SEQ) * rows, rows, 0)
    strip = strip.T.reshape(per, hi, rows // 128, 128).transpose(1, 2, 0, 3)
    strip = strip.reshape(hi, rows // 128 * per, 128)
    lo_rank = lax.axis_index("tp_lo")

    def both_cores(same):
        other = lax.ppermute(same, "seq_1", [(0, 1), (1, 0)])
        return same, other

    def from_ring(value, axis, step, pick):
        size = lax.axis_size(axis)
        parts = [pick(value, 0)]
        for k in range(1, size):
            route = [(i, (i + step * k) % size) for i in range(size)]
            parts.append(lax.ppermute(pick(value, k), axis, route))
        return jnp.stack(parts)

    cut = lax.dynamic_slice_in_dim(w_outp, lax.axis_index(SEQ) * lo * 128, lo * 128, 1)
    cut = cut.reshape(channels, lo, 128).transpose(1, 0, 2)

    def for_peer(value, k):
        return lax.dynamic_index_in_dim(value, (lo_rank + k) % lo, 0, keepdims=False)

    def chips_of(value):
        return from_ring(value, "seq_0", -1, lambda value, k: value)

    w_near = from_ring(cut, "tp_lo", 1, for_peer)

    place = jnp.stack([lo_rank, core, chip]).astype(jnp.int32)
    gain = gain.reshape(hi, lo, 128)
    w_step = jnp.pad(w_step.T, ((0, 16 - heads), (0, 0)))
    bias = jnp.pad(bias, (0, 128 - heads))[None]
    rates = jnp.pad(rates, (0, 128 - heads))[None]
    skip = jnp.repeat(skip_coef, HEAD_DIM)[None]
    o_gain = o_gain[None]

    def mixer(resid, weights):
        count = resid.shape[0]
        half = count // 2
        sent = jnp.broadcast_to(resid[None], (hi, *resid.shape))
        if weights is None:
            got = swap(jnp.concatenate([sent, strip], axis=1), "tp_hi")
            near = w_near
            far = got[:, :count]
            own = got[:, count:].reshape(hi, rows // 128, per, 128)
        else:
            far = swap(sent, "tp_hi")
            w_bc, w_out = weights
        behind = shifted(far, 1)
        ahead = shifted(far, -1)
        across_a = shifted(far[:, :half], 2)
        across_b = shifted(far[:, half:], -2)
        if weights is None:
            w_bc = chips_of(own)
            w_bc = both_cores(w_bc)

        def by_hi(rows_here):
            return pl.BlockSpec((2, rows_here, 128), lambda i, s: (i, 0, 0))

        strip_spec = pl.BlockSpec(
            (1, *w_bc[0].shape[1:]), lambda i, s: ((i + chips - s[2]) % chips, 0, 0, 0, 0)
        )
        tall = 2 * lo * 128
        outs = [
            ((lo, count, 128), BF),
            ((count, channels), F32),
            ((count, channels), F32),
            ((count, 128), F32),
            ((count, 128), F32),
            ((8, 128), F32),
        ]
        project = pl.pallas_call(
            project_kernel,
            out_shape=[jax.ShapeDtypeStruct(*o) for o in outs],
            grid_spec=pltpu.PrefetchScalarGridSpec(
                num_scalar_prefetch=1,
                grid=(hi // 2,),
                in_specs=[
                    by_hi(count),
                    by_hi(count),
                    by_hi(half),
                    by_hi(half),
                    by_hi(count),
                    pl.BlockSpec((2, lo, 128), lambda i, s: (i, 0, 0)),
                    pl.BlockSpec((tall, w_inp.shape[1]), lambda i, s: (i, 0)),
                    strip_spec,
                    strip_spec,
                    pl.BlockSpec((16, tall), lambda i, s: (0, i)),
                    whole((1, 128)),
                    whole((1, 128)),
                ],
                out_specs=[whole(o[0]) for o in outs],
                scratch_shapes=[
                    pltpu.VMEM((2, lo, count, 128), BF),
                    pltpu.VMEM((2, count, lo * 128), BF),
                    pltpu.VMEM((128, tall), BF),
                    pltpu.VMEM((count, w_inp.shape[1]), F32),
                    pltpu.VMEM((count, 128), F32),
                    pltpu.VMEM((count, 128), F32),
                    pltpu.VMEM((count, 1), F32),
                ],
            ),
            interpret=INTERPRET,
            name="project",
        )
        share, xs, gates, step, cum, total = project(
            place, far, ahead, across_a, across_b, behind, gain,
            w_inp, *w_bc, w_step, bias, rates
        )

        twin = lax.ppermute(total, "seq_1", [(0, 1), (1, 0)])
        shared = swap(share, "tp_lo")
        if weights is None:
            across = chips_of(near)
        depth = lo * here // 2
        sent, local, y, cmat, grow = run(
            piece_kernel,
            (shared, xs, step, cum, twin, skip),
            [
                ((chips, depth + 16, channels), BF),
                ((depth, channels), F32),
                ((count, channels), F32),
                ((count, depth), BF),
                ((count, channels), F32),
            ],
            place,
        )
        got = swap(sent, "seq_0")
        if weights is None:
            got, across = lax.optimization_barrier((got, across))
            w_out = both_cores(across)
        sent, keep = run(
            carry_kernel,
            (got, local),
            [((depth, channels), BF), ((depth, channels), F32)],
            place,
        )
        other = lax.ppermute(sent, "seq_1", [(0, 1), (1, 0)])
        (sent,) = run(
            gate_kernel,
            (other, keep, cmat, y, grow, gates, o_gain),
            [((lo, count + 16, channels), BF)],
        )
        got = swap(sent, "tp_lo")
        block = pl.BlockSpec((1, lo, channels, 128), lambda i: (i, 0, 0, 0))
        shares = pl.pallas_call(
            close_kernel,
            grid=(chips,),
            out_shape=jax.ShapeDtypeStruct((hi, count, 128), BF),
            in_specs=[SCALARS, whole(got.shape), block, block],
            out_specs=whole((hi, count, 128)),
            interpret=INTERPRET,
            name="close",
        )(place, got, *w_out)
        summed = jnp.sum(swap(shares, "tp_hi").astype(F32), axis=0)
        return (resid.astype(F32) + summed).astype(BF), (w_bc, w_out)

    opening, weights = mixer(waiting_batchlets[0], None)
    sections = lax.axis_size("section")
    moved = lax.ppermute(opening, "section", [(i, i + 1) for i in range(sections - 1)])
    second_in = jnp.where(lax.axis_index("section") == 0, arriving_batchlet, moved)
    return mixer(second_in, weights)[0][None]


def solution(mesh, cut=None):
    sections, seq, tp = (mesh.shape[name] for name in ("section", "seq", "tp"))
    near = cut or 4
    torus = Mesh(
        mesh.devices.reshape(sections, seq // 2, 2, tp // near, near),
        ("section", *SEQ, *TP),
    )
    return jax.shard_map(
        body,
        mesh=torus,
        in_specs=(
            P("section", SEQ, TP),
            P(SEQ, TP),
            P("section", None),
            P("section", None, TP),
            P("section", None, TP),
            P("section", TP),
            P("section", TP),
            P("section", None, TP),
            P("section", TP),
            P("section", TP),
            P("section", TP, None),
        ),
        out_specs=P("section", SEQ, TP),
        check_vma=False,
    )
```
